256 devices in a mesh: chan: 64 (over z, x, core), tile: 4 (over y).
Axes of the slice: x: 4, y: 4, z: 8, core: 2. Of those that a mesh axis runs over, the one named last changes fastest.
Arguments:
- gamma_pair: bfloat16 [64, 2048, 2048], P('chan', 'tile'), may hold values from -8 to 8, as said below
- energies: float32 [64, 2048], P('chan'), may hold values from 0.5 to 4
- occupancy: int32 [64, 2048], P('chan'), may hold values from 0 to 2
- recoup: bfloat16 [8, 128, 128], replicated, may hold values from -0.5 to 0.5
- recoup_class: int32 [64, 16, 16], P('chan', 'tile'), may hold values from 0 to 7
- send_slot: int32 [64, 16, 16], P('chan', 'tile'), may hold values from 0 to 63, as said below
- recv_slot: int32 [64, 16, 16], P('chan', 'tile'), may hold values from 0 to 63, as said below
Outputs:
- flowed: float32 [64, 2048, 2048], P('chan', 'tile')
The draws below stay inside these ranges and needn't reach their ends.
Inputs may be any that keep to these rules, and one draw needn't show every extreme that they name: gamma_pair is symmetric in its last two dimensions. `send_slot`: for each channel and block b, the 64 entries of tile rows b * 4 to (b + 1) * 4 - 1 are a permutation of 0 to 63; entry q = 1 * c + s with 0 <= s < 1 sends the tile to channel c in its slot s, so each channel receives exactly 1 tiles from each block of each channel. `recv_slot`: for each channel and block b, the 64 entries of tile rows b * 4 to (b + 1) * 4 - 1 are a permutation of 0 to 63; entry q = 1 * c + s with 0 <= s < 1 names the tile received from channel c in its slot s.
All inputs are finite; a program needn't handle non-finite values.
Results may differ from the reference program's by a relative error of at most 0.002.
Values may be sent and summed in bfloat16 or wider, within the bound.
No kernel may reach another device: no remote copies, remote signals or barrier semaphores. Data moves between devices by JAX's collectives and lax.ppermute only.
A program may use at most 128 MiB of HBM per device.

```python
import math
import jax
import jax.numpy as jnp
from jax import lax

W = 2048
TB = 128
NG = 8
NCH = 64
TR = 16
TRD = 4
TPD = 64
CAP = 1
N_CHAN = 64
N_TILE = 4


def draw_gamma_pair(key, part):
    normal_part = jax.random.normal(jax.random.fold_in(key, 3), (NCH, W, W), jnp.float32)
    symmetric = (normal_part + jnp.swapaxes(normal_part, 1, 2)) * 0.7071
    return jnp.clip(symmetric, -8.0, 8.0).astype(jnp.bfloat16)


def slot_table(key):
    scores = jax.random.randint(key, (NCH, TR // TRD, TPD), 0, 2 ** 20)
    scores = scores * TPD + jnp.arange(TPD, dtype=jnp.int32)[None, None, :]
    return jnp.argsort(scores, axis=-1).astype(jnp.int32).reshape(NCH, TR, TR)


def draw_send_slot(key, part):
    return slot_table(jax.random.fold_in(key, 11))


def draw_recv_slot(key, part):
    return slot_table(jax.random.fold_in(key, 23))


def place_ends(result, own_key, low, top_value):
    dims = result.shape
    spot = [jax.random.randint(jax.random.fold_in(own_key, axis), (), 0, dims[axis]) for axis in range(len(dims))]
    result = result.at[tuple(spot)].set(low)
    longest = dims.index(max(dims))
    spot[longest] = (spot[longest] + 1) % dims[longest]
    return result.at[tuple(spot)].set(top_value)


def levels(own_key, shape, shards, low, largest):
    loudness, own = 1.0, jax.random.fold_in(own_key, 6)
    for position, shards_of in shards:
        steps = jnp.exp(jax.random.uniform(jax.random.fold_in(own, position), (shards_of,), jnp.float32, low / len(shards), largest / len(shards)))
        loudness = loudness * jnp.repeat(steps, shape[position] // shards_of).reshape([-1 if axis == position else 1 for axis in range(len(shape))])
    return loudness


def normal_values(rng, shape, deviation, reach, held_as=jnp.bfloat16):
    result = deviation * jax.random.normal(rng, shape, jnp.float32)
    return jnp.clip(result, min=-reach, max=reach).astype(held_as)


def setup_inputs(seed: int = 0) -> dict:
    key_list = jax.random.split(jax.random.key(seed), 8)
    return {
        "gamma_pair": draw_gamma_pair(jax.random.fold_in(key_list[7], 71), 0),
        "energies": jnp.clip(jnp.exp(math.log(4.0) - 2.0794415 * jax.random.uniform(key_list[1], (NCH, W), jnp.float32) ** levels(key_list[1], (NCH, W), ((0, 64),), -0.2, 0.2)), 0.5, 4.0),
        "occupancy": place_ends(jax.random.randint(key_list[2], (NCH, W), 0, 3), jax.random.fold_in(key_list[2], 1), 0, 2).astype(jnp.int32),
        "recoup": normal_values(key_list[3], (NG, TB, TB), TB ** -0.5, 0.5),
        "recoup_class": place_ends(jax.random.randint(key_list[4], (NCH, TR, TR), 0, NG), jax.random.fold_in(key_list[4], 1), 0, NG - 1).astype(jnp.int32),
        "send_slot": draw_send_slot(jax.random.fold_in(key_list[7], 71), 0),
        "recv_slot": draw_recv_slot(jax.random.fold_in(key_list[7], 71), 0),
    }


def to_tiles(matrix):
    channels = matrix.shape[0]
    blocks = matrix.reshape(channels, N_TILE, TRD, TB, TR, TB)
    blocks = jnp.transpose(blocks, (0, 1, 2, 4, 3, 5))
    return blocks.reshape(channels, N_TILE, TPD, TB, TB)


def from_tiles(tile_set):
    channels = tile_set.shape[0]
    blocks = tile_set.reshape(channels, N_TILE, TRD, TR, TB, TB)
    blocks = jnp.transpose(blocks, (0, 1, 2, 4, 3, 5))
    return blocks.reshape(channels, W, W)


def pair_part(inputs):
    gamma_one, energy_one, occ_one = inputs
    occ_float = occ_one.astype(jnp.float32)
    upper_mask = ((occ_float[:, None] == 0.0) & (occ_float[None, :] == 2.0)).astype(jnp.float32)
    lower_mask = ((occ_float[:, None] == 2.0) & (occ_float[None, :] == 0.0)).astype(jnp.float32)
    denom = energy_one[:, None] + energy_one[None, :]
    eta_one = (gamma_one.astype(jnp.float32) * (upper_mask - lower_mask) / denom).astype(jnp.bfloat16)
    eta_scaled = eta_one * (1.0 - occ_float).astype(jnp.bfloat16)[None, :]
    ladder_half = jnp.dot(eta_scaled, gamma_one, preferred_element_type=jnp.float32)
    return eta_one, ladder_half + ladder_half.T


def cross_part(inputs):
    eta_cross, gamma_cross = inputs
    product = jnp.dot(eta_cross, gamma_cross, preferred_element_type=jnp.float32)
    return (product - product.T).astype(jnp.bfloat16)


def swap_groups(buffer):
    buffer = buffer.reshape(NCH, N_TILE, N_CHAN, CAP, TB, TB)
    buffer = jnp.transpose(buffer, (2, 1, 0, 3, 4, 5))
    return buffer.reshape(NCH, N_TILE, TPD, TB, TB)


def reference(gamma_pair, energies, occupancy, recoup, recoup_class, send_slot, recv_slot):
    eta_all, ladder = lax.map(pair_part, (gamma_pair, energies, occupancy))
    send_flat = send_slot.reshape(NCH, N_TILE, TPD)
    recv_flat = recv_slot.reshape(NCH, N_TILE, TPD)
    coeff_set = recoup[recoup_class.reshape(NCH, N_TILE, TPD)].astype(jnp.float32)

    def recouple(matrix):
        return jnp.einsum('cukab,cukbd->cukad', to_tiles(matrix).astype(jnp.float32), coeff_set).astype(jnp.bfloat16)

    def route_out(tile_set):
        sorter = jnp.argsort(send_flat, axis=-1).astype(jnp.int32)
        buffer = jnp.take_along_axis(tile_set, sorter[:, :, :, None, None], axis=2)
        buffer = swap_groups(buffer)
        return jnp.take_along_axis(buffer, recv_flat[:, :, :, None, None], axis=2)

    eta_cross = from_tiles(route_out(recouple(eta_all)))
    gamma_cross = from_tiles(route_out(recouple(gamma_pair)))
    cross_sym = lax.map(cross_part, (eta_cross, gamma_cross))
    sorter = jnp.argsort(recv_flat, axis=-1).astype(jnp.int32)
    buffer = jnp.take_along_axis(to_tiles(cross_sym), sorter[:, :, :, None, None], axis=2)
    buffer = swap_groups(buffer)
    pair_tiles = jnp.take_along_axis(buffer, send_flat[:, :, :, None, None], axis=2)
    back_tiles = jnp.einsum('cukab,cukdb->cukad', pair_tiles.astype(jnp.float32), coeff_set)
    back_full = from_tiles(back_tiles)
    step_size = float(W) ** -0.5
    return gamma_pair.astype(jnp.float32) + step_size * (ladder + back_full)
```

```python
import functools
import math

import jax
import jax.numpy as jnp
from jax import lax
from jax.experimental import pallas as pl
from jax.experimental.pallas import tpu as pltpu
from jax.sharding import PartitionSpec as P


BF = jnp.bfloat16
F32 = jnp.float32
TB = 128
META = 8
CHUNKS = 2
ROWS = TB // CHUNKS
SMEM = pl.BlockSpec(memory_space=pltpu.SMEM)
VMEM = pl.BlockSpec(memory_space=pltpu.VMEM)
ANY = pl.BlockSpec(memory_space=pl.ANY)
BIG = pltpu.CompilerParams(vmem_limit_bytes=60 << 20)


def coded(energy, occ):
    return jnp.where(occ == 0, energy, jnp.where(occ == 2, -energy, 0.0))


def pack_kernel(chunk, tiles_across, me, send, cls, gamma, energy, occ, buf, row_pieces, col_pieces):
    if chunk == 0:
        value = coded(energy[...], occ[...])
        first = value.astype(BF).astype(F32)
        rest = value - first
        second = rest.astype(BF).astype(F32)
        third = rest - second
        row_pieces[...] = jnp.zeros_like(row_pieces)
        col_pieces[...] = jnp.zeros_like(col_pieces)
        for n, piece in enumerate((first, second, third)):
            row_pieces[n : n + 1, :] = piece
            col_pieces[n + 3 : n + 4, :] = piece
    rows_down = gamma.shape[0] // TB

    def body(k, carry):
        i, j = k // tiles_across, k % tiles_across
        across = pl.ds(pl.multiple_of(j * TB, TB), TB)
        slot = send[i, j]
        buf[slot, 0:ROWS, :] = gamma[pl.ds(pl.multiple_of(i * TB + chunk * ROWS, ROWS), ROWS), across]
        if chunk == 0:
            down = pl.ds(pl.multiple_of((me[0] * rows_down + i) * TB, TB), TB)
            line = lax.broadcasted_iota(jnp.int32, (META, TB), 0)
            head = row_pieces[:, down] + col_pieces[:, across]
            head = head + jnp.where(line == 6, cls[i, j].astype(F32), 0.0)
            buf[slot, ROWS : ROWS + META, :] = head.astype(BF)
        return carry

    lax.fori_loop(0, rows_down * tiles_across, body, 0, unroll=8)


def pack(chunk, me, send, cls, gamma, energy, occ):
    rows = ROWS + (META if chunk == 0 else 0)
    return pl.pallas_call(
        functools.partial(pack_kernel, chunk, gamma.shape[1] // TB),
        out_shape=jax.ShapeDtypeStruct((send.size, rows, TB), BF),
        in_specs=[SMEM] * 3 + [VMEM] * 3,
        out_specs=VMEM,
        scratch_shapes=[pltpu.VMEM((META, gamma.shape[1]), F32)] * 2,
    )(me, send, cls, gamma, energy, occ)


def tables_kernel(own, right, far, left, out):
    for n, table in enumerate((own, right, far, left)):
        out[n] = table[...]


def join_tables(*tables):
    return pl.pallas_call(
        tables_kernel,
        out_shape=jax.ShapeDtypeStruct((4,) + tables[0].shape, jnp.int32),
        in_specs=[VMEM] * 4,
        out_specs=VMEM,
        name="join_tables",
    )(*tables)


def share_kernel(me, gamma, right, left):
    side = gamma.shape[0]
    half = side // 2

    def block(offset):
        return pl.ds(pl.multiple_of(((me[0] + offset) % 4) * side, side), side)

    own = gamma[:, block(0)]
    right[0:side, :] = own
    left[0:side, :] = own
    right[side : 2 * side, :] = gamma[:, block(3)]
    left[side : 2 * side, :] = gamma[:, block(1)]
    far = gamma[:, block(2)]
    right[2 * side :, :] = far[0:half]
    left[2 * side :, 0:half] = far[0:half, half:]
    left[2 * side :, half:] = far[half:, half:]


def share(me, gamma):
    side = gamma.shape[0]
    shape = jax.ShapeDtypeStruct((2 * side + side // 2, side), BF)
    return pl.pallas_call(
        share_kernel,
        out_shape=[shape, shape],
        in_specs=[SMEM, VMEM],
        out_specs=[VMEM, VMEM],
        name="share_blocks",
    )(me, gamma)


def ladder_kernel(step_size, me, gamma, from_left, from_right, far_a, far_b, energy, occ, base, full, scaled, column):
    side = gamma.shape[0]
    half = side // 2
    width = gamma.shape[1]

    def put(a, b, value, row=0, col=0):
        rows = pl.ds(pl.multiple_of(((me[0] + a) % 4) * side + row, half), value.shape[0])
        cols = pl.ds(pl.multiple_of(((me[0] + b) % 4) * side + col, half), value.shape[1])
        full[rows, cols] = value

    def turn(value):
        return jnp.transpose(value.astype(F32)).astype(BF)

    mine = pl.ds(pl.multiple_of(me[0] * side, side), side)
    full[mine, :] = gamma[...]
    for b in range(1, 4):
        cols = pl.ds(pl.multiple_of(((me[0] + b) % 4) * side, side), side)
        put(b, 0, turn(gamma[:, cols]))
    put(3, 3, from_left[0:side, :])
    put(3, 2, from_left[side : 2 * side, :])
    put(2, 3, turn(from_left[side : 2 * side, :]))
    put(3, 1, from_left[2 * side :, :])
    put(1, 3, turn(from_left[2 * side :, :]))
    put(1, 1, from_right[0:side, :])
    put(1, 2, from_right[side : 2 * side, :])
    put(2, 1, turn(from_right[side : 2 * side, :]))
    for n in range(2):
        piece = from_right[2 * side :, n * half : (n + 1) * half]
        put(1, 3, piece, row=n * half, col=half)
        put(3, 1, turn(piece), row=half, col=n * half)
    put(2, 2, far_a[...])
    put(2, 2, far_b[...], row=half)

    value = coded(energy[...], occ[...])
    column[...] = jnp.transpose(jnp.broadcast_to(value, (8, width)))

    def scale(n, carry):
        rows = pl.ds(pl.multiple_of(n * 64, 64), 64)
        down = column[rows, 0:1]
        ratio = -full[rows, :].astype(F32) / jnp.abs(down - value)
        scaled[rows, :] = jnp.where(down * value < 0.0, ratio, 0.0).astype(BF)
        return carry

    lax.fori_loop(0, width // 64, scale, 0)

    def product(n, carry):
        cols = pl.ds(pl.multiple_of(n * 256, 256), 256)
        total = jnp.dot(scaled[mine, :], full[:, cols], preferred_element_type=F32)
        total = total + jnp.dot(full[mine, :], scaled[:, cols], preferred_element_type=F32)
        base[:, cols] = gamma[:, cols].astype(F32) + step_size * total
        return carry

    lax.fori_loop(0, width // 256, product, 0)


def ladder_base(step_size, me, gamma, from_left, from_right, far_a, far_b, energy, occ):
    width = gamma.shape[1]
    return pl.pallas_call(
        functools.partial(ladder_kernel, step_size),
        out_shape=jax.ShapeDtypeStruct(gamma.shape, F32),
        in_specs=[SMEM] + [VMEM] * 7,
        out_specs=VMEM,
        scratch_shapes=[
            pltpu.VMEM((width, width), BF),
            pltpu.VMEM((width, width), BF),
            pltpu.VMEM((width, 8), F32),
        ],
        compiler_params=BIG,
        name="ladder",
    )(me, gamma, from_left, from_right, far_a, far_b, energy, occ)


def decode(head, picks, down, along, cls, cls_int, sem):
    count = down.shape[1]
    lines = jnp.dot(picks[...], head, preferred_element_type=F32)
    side = jnp.concatenate([lines[0:count], jnp.zeros((TB - count, TB), F32)], axis=0) if count < TB else lines[0:count]
    down[...] = jnp.transpose(side)[:, 0:count]
    along[...] = lines[count : 2 * count]
    cls_int[...] = lines[2 * count :].astype(jnp.int32)
    copy = pltpu.make_async_copy(cls_int, cls, sem)
    copy.start()
    copy.wait()


def fill_picks(picks, count):
    row = lax.broadcasted_iota(jnp.int32, picks.shape, 0)
    col = lax.broadcasted_iota(jnp.int32, picks.shape, 1)
    kind, line = row // count, col % META
    hit = ((kind == 2) & (line == 6)) | ((kind < 2) & (line >= 3 * kind) & (line < 3 * kind + 3))
    picks[...] = jnp.where((col // META == row % count) & hit, 1.0, 0.0).astype(BF)


def recouple_block(chunk, across, raw, block, recv, recoup, scratch, put):
    down, along, cls, eta = scratch
    count = raw.shape[0]
    for q in range(count):
        column = down[chunk * ROWS : (chunk + 1) * ROWS, q : q + 1]
        line = along[q : q + 1, :]
        ratio = raw[q].astype(F32) / (column - line)
        eta[q] = jnp.where(column * line < 0.0, ratio, 0.0).astype(BF)

    def body(p, carry):
        i, j = p // across, p % across
        q = recv[block, i, j]
        both = jnp.concatenate([eta[q], raw[q]], axis=0)
        done = jnp.dot(both, recoup[cls[q, 0]], preferred_element_type=F32).astype(BF)
        put(i, pl.ds(pl.multiple_of(j * TB, TB), TB), done[0:ROWS], done[ROWS:])
        return carry

    lax.fori_loop(0, count, body, 0, unroll=8)


def block_scratch(groups, count):
    return [
        pltpu.VMEM((groups, count, ROWS, TB), BF),
        pltpu.VMEM((groups, count, META, TB), BF),
        pltpu.VMEM((3 * count, count * META), BF),
        pltpu.VMEM((TB, count), F32),
        pltpu.VMEM((count, TB), F32),
        pltpu.VMEM((count, TB), jnp.int32),
        pltpu.SMEM((count, TB), jnp.int32),
        pltpu.VMEM((count, ROWS, TB), BF),
        pltpu.SemaphoreType.DMA((groups, 5)),
    ]


def waits(raws, heads, raw, head, sems):
    copies, start = [], 0
    for n, (source, top) in enumerate(zip(raws, heads)):
        where = pl.ds(start, source.shape[0])
        start += source.shape[0]
        copies.append(pltpu.make_async_copy(top.at[:, ROWS : ROWS + META, :], head.at[where], sems.at[2 * n + 1]))
        copies.append(pltpu.make_async_copy(source.at[:, 0:ROWS, :], raw.at[where], sems.at[2 * n]))
    return copies


def fetch(*refs):
    copies = waits(*refs)
    for copy in copies:
        copy.start()
    return copies


def recouple_kernel(chunk, across, parts, blocks, recv, recoup, *refs):
    total = parts * len(blocks)
    raws, heads, refs = refs[:total], refs[total : 2 * total], refs[2 * total :]
    eta_out, gamma_out, raw, head, picks, down, along, cls_int, cls, eta, sems = refs
    for n in range(len(blocks)):
        span = slice(n * parts, (n + 1) * parts)
        fetch(raws[span], heads[span], raw.at[n], head.at[n], sems.at[n])
    count = raw.shape[1]
    high = eta_out.shape[0] // len(blocks)
    fill_picks(picks, count)

    def group(n, carry):
        block = sum(jnp.where(n == k, b, 0) for k, b in enumerate(blocks))
        for copy in waits(raws[:parts], heads[:parts], raw.at[n], head.at[n], sems.at[n]):
            copy.wait()
        decode(head[n].reshape(count * META, TB), picks, down, along, cls, cls_int, sems.at[n, 4])

        def put(i, cols, eta_tile, gamma_tile):
            eta_out[n * high + i, :, cols] = eta_tile
            gamma_out[n * high + i, :, cols] = gamma_tile

        recouple_block(chunk, across, raw.at[n], block, recv, recoup, (down, along, cls, eta), put)
        return carry

    lax.fori_loop(0, len(blocks), group, 0)


def recouple(chunk, across, blocks, tables, recoup, raws, heads):
    parts = len(raws[0])
    count = sum(raw.shape[0] for raw in raws[0])
    shape = jax.ShapeDtypeStruct((len(blocks) * count // across, ROWS, across * TB), BF)
    return pl.pallas_call(
        functools.partial(recouple_kernel, chunk, across, parts, blocks),
        out_shape=[shape, shape],
        in_specs=[SMEM, VMEM] + [ANY] * (2 * parts * len(blocks)),
        out_specs=[VMEM, VMEM],
        scratch_shapes=block_scratch(len(blocks), count),
        compiler_params=BIG,
    )(tables, recoup, *[r for group in raws for r in group], *[r for group in heads for r in group])


def cross_kernel(chunk, blocks, parts, me, recv, recoup, *refs):
    groups = len(set(key for _, _, key, _ in blocks))
    pieces, refs = refs[: 2 * groups], refs[2 * groups :]
    raws, heads, refs = refs[:parts], refs[parts : 2 * parts], refs[2 * parts :]
    out, eta, gamma, turned, piece_sems = refs[:5]
    raw, head, picks, down, along, cls_int, cls, eta_raw, sems = refs[5:]
    rows_down = recv.shape[1]
    width = pieces[0].shape[2]
    late = fetch(raws, heads, raw.at[0], head.at[0], sems.at[0])
    copies = []
    for n, (part, block, key, place) in enumerate(blocks):
        where = pl.ds(((me[0] + block) % 4) * rows_down, rows_down)
        for which, target in enumerate((eta, gamma)):
            source = pieces[2 * key + which].at[pl.ds(place * rows_down, rows_down)]
            into = target.at[where, pl.ds(part * ROWS, ROWS), :]
            copies.append(pltpu.make_async_copy(source, into, piece_sems.at[2 * n + which]))
    for copy in copies:
        copy.start()
    count = raw.shape[1]
    fill_picks(picks, count)
    for copy in late:
        copy.wait()
    decode(head[0].reshape(count * META, TB), picks, down, along, cls, cls_int, sems.at[0, 4])
    far = ((me[0] + 2) % 4) * rows_down

    def put(i, cols, eta_tile, gamma_tile):
        eta[far + i, chunk * ROWS : (chunk + 1) * ROWS, cols] = eta_tile
        gamma[far + i, chunk * ROWS : (chunk + 1) * ROWS, cols] = gamma_tile

    recouple_block(chunk, width // TB, raw.at[0], 2, recv, recoup, (down, along, cls, eta_raw), put)
    for copy in copies:
        copy.wait()
    side = rows_down * TB
    mine = pl.ds(me[0] * rows_down, rows_down)
    for i in range(rows_down):
        cols = pl.ds(pl.multiple_of((me[0] * rows_down + i) * TB, TB), TB)
        for k in range(4 * rows_down):
            tile = gamma[k, :, cols].astype(F32)
            turned[i * TB : (i + 1) * TB, k * TB : (k + 1) * TB] = jnp.transpose(tile).astype(BF)
    step = 2

    def body(n, carry):
        cols = pl.ds(pl.multiple_of(n * step * TB, step * TB), step * TB)
        half = jnp.dot(
            eta[mine].reshape(side, width),
            gamma[:, :, cols].reshape(width, step * TB),
            preferred_element_type=F32,
        )
        other = lax.dot_general(
            turned[...],
            eta[pl.ds(n * step, step)].reshape(step * TB, width),
            (((1,), (1,)), ((), ())),
            preferred_element_type=F32,
        )
        result = (half - other).astype(BF)
        for i in range(rows_down):
            for j in range(step):
                out[recv[0, i, n * step + j]] = result[i * TB : (i + 1) * TB, j * TB : (j + 1) * TB]
        return carry

    lax.fori_loop(0, width // (step * TB), body, 0)


def cross(chunk, me, tables, recoup, pieces, raws, heads):
    flat = [array for _, _, pair in pieces for array in pair]
    blocks = tuple(
        (part, block, key, place)
        for key, (part, members, _) in enumerate(pieces)
        for place, block in enumerate(members)
    )
    rows_down, width = tables.shape[1], flat[0].shape[2]
    return pl.pallas_call(
        functools.partial(cross_kernel, chunk, blocks, len(raws)),
        out_shape=jax.ShapeDtypeStruct((tables[0].size, TB, TB), BF),
        in_specs=[SMEM] * 2 + [VMEM] + [ANY] * (len(flat) + 2 * len(raws)),
        out_specs=VMEM,
        scratch_shapes=[
            pltpu.VMEM((4 * rows_down, TB, width), BF),
            pltpu.VMEM((4 * rows_down, TB, width), BF),
            pltpu.VMEM((rows_down * TB, width), BF),
            pltpu.SemaphoreType.DMA((2 * len(blocks),)),
        ]
        + block_scratch(1, tables[0].size),
        compiler_params=BIG,
        name="cross",
    )(me, tables, recoup, *flat, *raws, *heads)


def final_kernel(step_size, send, cls, base, back, recoup, out):
    i = pl.program_id(0)
    for j in range(base.shape[1] // TB):
        cols = slice(j * TB, (j + 1) * TB)
        turned = lax.dot_general(
            back[send[i, j]], recoup[cls[i, j]], (((1,), (1,)), ((), ())), preferred_element_type=F32
        )
        out[:, cols] = base[:, cols] + step_size * turned


def finish(step_size, send, cls, base, back, recoup):
    width = base.shape[1]
    rows = pl.BlockSpec((TB, width), lambda i: (i, 0))
    return pl.pallas_call(
        functools.partial(final_kernel, step_size),
        grid=(base.shape[0] // TB,),
        out_shape=jax.ShapeDtypeStruct(base.shape, F32),
        in_specs=[
            SMEM,
            SMEM,
            rows,
            pl.BlockSpec(back.shape, lambda i: (0, 0, 0)),
            pl.BlockSpec(recoup.shape, lambda i: (0, 0, 0)),
        ],
        out_specs=rows,
        name="finish",
    )(send, cls, base, back, recoup)


RIGHT = [(i, (i + 1) % 4) for i in range(4)]
LEFT = [(i, (i + 3) % 4) for i in range(4)]
ACROSS = [(i, (i + 2) % 4) for i in range(4)]


def on_device(gamma_pair, energies, occupancy, recoup, recoup_class, send_slot, recv_slot):
    gamma = gamma_pair[0]
    width = gamma.shape[1]
    across = width // TB
    step_size = 1.0 / math.sqrt(width)
    me = lax.axis_index("tile").astype(jnp.int32).reshape(1)
    send, recv, cls = send_slot[0], recv_slot[0], recoup_class[0]

    arrived = []
    for h in range(CHUNKS):
        buf = pack(h, me, send, cls, gamma, energies, occupancy)
        arrived.append(lax.all_to_all(buf, "chan", split_axis=0, concat_axis=0, tiled=True))
    to_right, to_left = share(me, gamma)
    half = gamma.shape[0] // 2
    from_left = lax.ppermute(to_right, "tile", RIGHT)
    from_right = lax.ppermute(to_left, "tile", LEFT)
    far_a = lax.ppermute(from_left[0:half], "tile", RIGHT)
    far_b = lax.ppermute(from_right[half : 2 * half], "tile", LEFT)
    tables = join_tables(
        recv,
        lax.ppermute(recv, "tile", LEFT),
        lax.ppermute(recv, "tile", ACROSS),
        lax.ppermute(recv, "tile", RIGHT),
    )
    base = ladder_base(step_size, me, gamma, from_left, from_right, far_a, far_b, energies, occupancy)

    pieces, heads = [], None

    def form(chunk, members, raws, tops):
        pieces.append((chunk, members, recouple(chunk, across, members, tables, recoup, raws, tops)))

    for h in range(CHUNKS):
        own = arrived[h]
        mid = own.shape[0] // 2
        left = lax.ppermute(own, "tile", RIGHT)
        right = lax.ppermute(own, "tile", LEFT)
        opposite = [lax.ppermute(left[0:mid], "tile", RIGHT), lax.ppermute(right[mid:], "tile", LEFT)]
        if h == 0:
            heads = ([own], [right], opposite, [left])
        if h + 1 < CHUNKS:
            form(h, (0, 1, 3), ([own], [right], [left]), (heads[0], heads[1], heads[3]))
            form(h, (2,), (opposite,), (heads[2],))
        else:
            form(h, (0,), ([own],), (heads[0],))
            form(h, (1, 3), ([right], [left]), (heads[1], heads[3]))
    crossed = cross(CHUNKS - 1, me, tables, recoup, pieces, opposite, heads[2])
    back = lax.all_to_all(crossed, "chan", split_axis=0, concat_axis=0, tiled=True)
    return finish(step_size, send, cls, base, back, recoup)[None]


def solution(mesh):
    placed = (
        P("chan", "tile", None),
        P("chan", None),
        P("chan", None),
        P(),
        P("chan", "tile", None),
        P("chan", "tile", None),
        P("chan", "tile", None),
    )
    return jax.shard_map(
        on_device, mesh=mesh, in_specs=placed, out_specs=P("chan", "tile", None), check_vma=False
    )
```

```python
import functools
import math

import jax
import jax.numpy as jnp
from jax import lax
from jax.experimental import pallas as pl
from jax.experimental.pallas import tpu as pltpu
from jax.sharding import PartitionSpec as P


BF = jnp.bfloat16
F32 = jnp.float32
TB = 128
META = 8
CHUNKS = 2
ROWS = TB // CHUNKS
SMEM = pl.BlockSpec(memory_space=pltpu.SMEM)
VMEM = pl.BlockSpec(memory_space=pltpu.VMEM)
ANY = pl.BlockSpec(memory_space=pltpu.HBM)
BIG = pltpu.CompilerParams(vmem_limit_bytes=60 << 20)


def coded(energy, occ):
    return jnp.where(occ == 0, energy, jnp.where(occ == 2, -energy, 0.0))


def pack_kernel(chunk, tiles_across, me, send, cls, gamma, energy, occ, buf, row_pieces, col_pieces):
    if chunk == 0:
        value = coded(energy[...], occ[...])
        first = value.astype(BF).astype(F32)
        rest = value - first
        second = rest.astype(BF).astype(F32)
        third = rest - second
        row_pieces[...] = jnp.zeros_like(row_pieces)
        col_pieces[...] = jnp.zeros_like(col_pieces)
        for n, piece in enumerate((first, second, third)):
            row_pieces[n : n + 1, :] = piece
            col_pieces[n + 3 : n + 4, :] = piece
    rows_down = gamma.shape[0] // TB

    def body(k, carry):
        i, j = k // tiles_across, k % tiles_across
        across = pl.ds(pl.multiple_of(j * TB, TB), TB)
        slot = send[i, j]
        buf[slot, 0:ROWS, :] = gamma[pl.ds(pl.multiple_of(i * TB + chunk * ROWS, ROWS), ROWS), across]
        if chunk == 0:
            down = pl.ds(pl.multiple_of((me[0] * rows_down + i) * TB, TB), TB)
            line = lax.broadcasted_iota(jnp.int32, (META, TB), 0)
            head = row_pieces[:, down] + col_pieces[:, across]
            head = head + jnp.where(line == 6, cls[i, j].astype(F32), 0.0)
            buf[slot, ROWS : ROWS + META, :] = head.astype(BF)
        return carry

    lax.fori_loop(0, rows_down * tiles_across, body, 0, unroll=8)


def pack(chunk, me, send, cls, gamma, energy, occ):
    rows = ROWS + (META if chunk == 0 else 0)
    return pl.pallas_call(
        functools.partial(pack_kernel, chunk, gamma.shape[1] // TB),
        out_shape=jax.ShapeDtypeStruct((send.size, rows, TB), BF),
        in_specs=[SMEM] * 3 + [VMEM] * 3,
        out_specs=VMEM,
        scratch_shapes=[pltpu.VMEM((META, gamma.shape[1]), F32)] * 2,
    )(me, send, cls, gamma, energy, occ)


def tables_kernel(own, right, far, left, out):
    across = own.shape[1]
    for n, table in enumerate((own, right, far, left)):

        def body(p, carry, n=n, table=table):
            out[n, table[p // across, p % across]] = p
            return carry

        lax.fori_loop(0, own.shape[0] * across, body, 0, unroll=8)


def place_tables(*tables):
    return pl.pallas_call(
        tables_kernel,
        out_shape=jax.ShapeDtypeStruct((4, tables[0].size), jnp.int32),
        in_specs=[SMEM] * 4,
        out_specs=SMEM,
        name="place_tables",
    )(*tables)


def share_kernel(me, gamma, right, left):
    side = gamma.shape[0]
    half = side // 2

    def block(offset):
        return pl.ds(pl.multiple_of(((me[0] + offset) % 4) * side, side), side)

    own = gamma[:, block(0)]
    right[0:side, :] = own
    left[0:side, :] = own
    right[side : 2 * side, :] = gamma[:, block(3)]
    left[side : 2 * side, :] = gamma[:, block(1)]
    far = gamma[:, block(2)]
    right[2 * side :, :] = far[0:half]
    left[2 * side :, 0:half] = far[0:half, half:]
    left[2 * side :, half:] = far[half:, half:]


def share(me, gamma):
    side = gamma.shape[0]
    shape = jax.ShapeDtypeStruct((2 * side + side // 2, side), BF)
    return pl.pallas_call(
        share_kernel,
        out_shape=[shape, shape],
        in_specs=[SMEM, VMEM],
        out_specs=[VMEM, VMEM],
        name="share_blocks",
    )(me, gamma)


def ladder_kernel(step_size, me, gamma, from_left, from_right, far_a, far_b, energy, occ, base, full, scaled, column):
    side = gamma.shape[0]
    half = side // 2
    width = gamma.shape[1]

    def put(a, b, value, row=0, col=0):
        rows = pl.ds(pl.multiple_of(((me[0] + a) % 4) * side + row, half), value.shape[0])
        cols = pl.ds(pl.multiple_of(((me[0] + b) % 4) * side + col, half), value.shape[1])
        full[rows, cols] = value

    def turn(value):
        return jnp.transpose(value.astype(F32)).astype(BF)

    mine = pl.ds(pl.multiple_of(me[0] * side, side), side)
    full[mine, :] = gamma[...]
    for b in range(1, 4):
        cols = pl.ds(pl.multiple_of(((me[0] + b) % 4) * side, side), side)
        put(b, 0, turn(gamma[:, cols]))
    put(3, 3, from_left[0:side, :])
    put(3, 2, from_left[side : 2 * side, :])
    put(2, 3, turn(from_left[side : 2 * side, :]))
    put(3, 1, from_left[2 * side :, :])
    put(1, 3, turn(from_left[2 * side :, :]))
    put(1, 1, from_right[0:side, :])
    put(1, 2, from_right[side : 2 * side, :])
    put(2, 1, turn(from_right[side : 2 * side, :]))
    for n in range(2):
        piece = from_right[2 * side :, n * half : (n + 1) * half]
        put(1, 3, piece, row=n * half, col=half)
        put(3, 1, turn(piece), row=half, col=n * half)
    put(2, 2, far_a[...])
    put(2, 2, far_b[...], row=half)

    value = coded(energy[...], occ[...])
    column[...] = jnp.transpose(jnp.broadcast_to(value, (8, width)))

    def scale(n, carry):
        rows = pl.ds(pl.multiple_of(n * 64, 64), 64)
        down = column[rows, 0:1]
        ratio = -full[rows, :].astype(F32) / jnp.abs(down - value)
        scaled[rows, :] = jnp.where(down * value < 0.0, ratio, 0.0).astype(BF)
        return carry

    lax.fori_loop(0, width // 64, scale, 0)

    def product(n, carry):
        cols = pl.ds(pl.multiple_of(n * 256, 256), 256)
        total = jnp.dot(scaled[mine, :], full[:, cols], preferred_element_type=F32)
        total = total + jnp.dot(full[mine, :], scaled[:, cols], preferred_element_type=F32)
        base[:, cols] = gamma[:, cols].astype(F32) + step_size * total
        return carry

    lax.fori_loop(0, width // 256, product, 0)


def ladder_base(step_size, me, gamma, from_left, from_right, far_a, far_b, energy, occ):
    width = gamma.shape[1]
    return pl.pallas_call(
        functools.partial(ladder_kernel, step_size),
        out_shape=jax.ShapeDtypeStruct(gamma.shape, F32),
        in_specs=[SMEM] + [VMEM] * 7,
        out_specs=VMEM,
        scratch_shapes=[
            pltpu.VMEM((width, width), BF),
            pltpu.VMEM((width, width), BF),
            pltpu.VMEM((width, 8), F32),
        ],
        compiler_params=BIG,
        name="ladder",
    )(me, gamma, from_left, from_right, far_a, far_b, energy, occ)


def fill_picks(picks, count):
    row = lax.broadcasted_iota(jnp.int32, picks.shape, 0)
    col = lax.broadcasted_iota(jnp.int32, picks.shape, 1)
    kind, line = row // count, col % META
    hit = ((kind == 2) & (line == 6)) | ((kind < 2) & (line >= 3 * kind) & (line < 3 * kind + 3))
    picks[...] = jnp.where((col // META == row % count) & hit, 1.0, 0.0).astype(BF)


def decode(head, picks, down, along, cls):
    count = along.shape[0]
    lines = jnp.dot(picks[...], head, preferred_element_type=F32)
    turned = jnp.transpose(jnp.concatenate([lines[0:count], lines[2 * count :]], axis=0))
    down[...] = turned
    along[...] = lines[count : 2 * count]
    cls[...] = turned[0:META].astype(jnp.int32)


def recouple_block(chunk, across, raw, down, along, cls, places, block, recoup, put):
    count = raw.shape[0]
    for q in range(count):
        column = down[chunk * ROWS : (chunk + 1) * ROWS, q : q + 1]
        line = along[q : q + 1, :]
        tile = raw[q]
        ratio = tile.astype(F32) / (column - line)
        eta = jnp.where(column * line < 0.0, ratio, 0.0).astype(BF)
        both = jnp.concatenate([eta, tile], axis=0)
        done = jnp.dot(both, recoup[cls(q)], preferred_element_type=F32).astype(BF)
        p = places[block, q]
        put(p // across, pl.ds(pl.multiple_of((p % across) * TB, TB), TB), done[0:ROWS], done[ROWS:])


def body_copies(raws, raw, sems):
    copies, start = [], 0
    for n, source in enumerate(raws):
        where = pl.ds(start, source.shape[0])
        start += source.shape[0]
        copies.append(pltpu.make_async_copy(source.at[:, 0:ROWS, :], raw.at[where], sems.at[n]))
    return copies


def head_copies(raws, head, sems):
    copies, start = [], 0
    for n, source in enumerate(raws):
        where = pl.ds(start, source.shape[0])
        start += source.shape[0]
        copies.append(pltpu.make_async_copy(source.at[:, ROWS : ROWS + META, :], head.at[where], sems.at[n]))
    return copies


def recouple_kernel(chunk, across, parts, blocks, places, recoup, *refs):
    groups = len(blocks)
    total = parts * groups
    raws, refs = refs[:total], refs[total:]
    if chunk == 0:
        eta_out, gamma_out, down, along, cls_int, raw, sems, head, picks, cls, head_sems = refs
    else:
        down, along, cls, eta_out, gamma_out, raw, sems = refs
    for n in range(groups):
        mine = raws[n * parts : (n + 1) * parts]
        if chunk == 0:
            for copy in head_copies(mine, head.at[n], head_sems.at[n]):
                copy.start()
        for copy in body_copies(mine, raw.at[n], sems.at[n]):
            copy.start()
    count = raw.shape[1]
    high = eta_out.shape[0] // groups
    if chunk == 0:
        fill_picks(picks, count)
        for n in range(groups):
            for copy in head_copies(raws[n * parts : (n + 1) * parts], head.at[n], head_sems.at[n]):
                copy.wait()
            decode(head[n].reshape(count * META, TB), picks, down.at[n], along.at[n], cls_int.at[n])
        copy = pltpu.make_async_copy(cls_int, cls, head_sems.at[0, 0])
        copy.start()
        copy.wait()

    def group(n, carry):
        block = sum(jnp.where(n == k, b, 0) for k, b in enumerate(blocks))
        for copy in body_copies(raws[:parts], raw.at[n], sems.at[n]):
            copy.wait()

        def put(i, cols, eta_tile, gamma_tile):
            eta_out[n * high + i, :, cols] = eta_tile
            gamma_out[n * high + i, :, cols] = gamma_tile

        recouple_block(
            chunk, across, raw.at[n], down.at[n], along.at[n], lambda q: cls[n, 0, count + q], places, block, recoup, put
        )
        return carry

    lax.fori_loop(0, groups, group, 0)


def recouple(chunk, across, blocks, places, recoup, raws, codes):
    groups, parts = len(blocks), len(raws[0])
    count = sum(raw.shape[0] for raw in raws[0])
    shapes = [jax.ShapeDtypeStruct((groups * count // across, ROWS, across * TB), BF)] * 2
    in_specs = [SMEM, VMEM] + [ANY] * (parts * groups)
    scratch = [pltpu.VMEM((groups, count, ROWS, TB), BF), pltpu.SemaphoreType.DMA((groups, parts))]
    if chunk == 0:
        shapes += [
            jax.ShapeDtypeStruct((groups, TB, 2 * count), F32),
            jax.ShapeDtypeStruct((groups, count, TB), F32),
            jax.ShapeDtypeStruct((groups, META, 2 * count), jnp.int32),
        ]
        scratch += [
            pltpu.VMEM((groups, count, META, TB), BF),
            pltpu.VMEM((3 * count, count * META), BF),
            pltpu.SMEM((groups, META, 2 * count), jnp.int32),
            pltpu.SemaphoreType.DMA((groups, parts)),
        ]
    else:
        in_specs += [VMEM, VMEM, SMEM]
    outs = pl.pallas_call(
        functools.partial(recouple_kernel, chunk, across, parts, blocks),
        out_shape=shapes,
        in_specs=in_specs,
        out_specs=[VMEM] * len(shapes),
        scratch_shapes=scratch,
        compiler_params=BIG,
    )(places, recoup, *[r for group in raws for r in group], *codes)
    return outs[0:2], outs[2:]


def cross_kernel(chunk, blocks, parts, me, recv, places, cls, recoup, down, along, *refs):
    groups = len(set(key for _, _, key, _ in blocks))
    pieces, refs = refs[: 2 * groups], refs[2 * groups :]
    raws, refs = refs[:parts], refs[parts:]
    out, eta, gamma, turned, piece_sems, raw, sems = refs
    rows_down = recv.shape[0]
    width = pieces[0].shape[2]
    late = body_copies(raws, raw, sems)
    copies = []
    for n, (part, block, key, place) in enumerate(blocks):
        where = pl.ds(((me[0] + block) % 4) * rows_down, rows_down)
        for which, target in enumerate((eta, gamma)):
            source = pieces[2 * key + which].at[pl.ds(place * rows_down, rows_down)]
            into = target.at[where, pl.ds(part * ROWS, ROWS), :]
            copies.append(pltpu.make_async_copy(source, into, piece_sems.at[2 * n + which]))
    for copy in late + copies:
        copy.start()
    for copy in late:
        copy.wait()
    count = raw.shape[0]
    far = ((me[0] + 2) % 4) * rows_down

    def put(i, cols, eta_tile, gamma_tile):
        eta[far + i, chunk * ROWS : (chunk + 1) * ROWS, cols] = eta_tile
        gamma[far + i, chunk * ROWS : (chunk + 1) * ROWS, cols] = gamma_tile

    recouple_block(
        chunk, width // TB, raw, down.at[0], along.at[0], lambda q: cls[0, 0, count + q], places, 2, recoup, put
    )
    for copy in copies:
        copy.wait()
    side = rows_down * TB
    mine = pl.ds(me[0] * rows_down, rows_down)
    for i in range(rows_down):
        cols = pl.ds(pl.multiple_of((me[0] * rows_down + i) * TB, TB), TB)
        for k in range(4 * rows_down):
            tile = gamma[k, :, cols].astype(F32)
            turned[i * TB : (i + 1) * TB, k * TB : (k + 1) * TB] = jnp.transpose(tile).astype(BF)
    step = 2

    def body(n, carry):
        cols = pl.ds(pl.multiple_of(n * step * TB, step * TB), step * TB)
        half = jnp.dot(
            eta[mine].reshape(side, width),
            gamma[:, :, cols].reshape(width, step * TB),
            preferred_element_type=F32,
        )
        other = lax.dot_general(
            turned[...],
            eta[pl.ds(n * step, step)].reshape(step * TB, width),
            (((1,), (1,)), ((), ())),
            preferred_element_type=F32,
        )
        result = (half - other).astype(BF)
        for i in range(rows_down):
            for j in range(step):
                out[recv[i, n * step + j]] = result[i * TB : (i + 1) * TB, j * TB : (j + 1) * TB]
        return carry

    lax.fori_loop(0, width // (step * TB), body, 0)


def cross(chunk, me, recv, places, recoup, pieces, raws, codes):
    flat = [array for _, _, pair in pieces for array in pair]
    blocks = tuple(
        (part, block, key, place)
        for key, (part, members, _) in enumerate(pieces)
        for place, block in enumerate(members)
    )
    rows_down, width = recv.shape[0], flat[0].shape[2]
    down, along, cls = codes
    return pl.pallas_call(
        functools.partial(cross_kernel, chunk, blocks, len(raws)),
        out_shape=jax.ShapeDtypeStruct((recv.size, TB, TB), BF),
        in_specs=[SMEM] * 4 + [VMEM] * 3 + [ANY] * (len(flat) + len(raws)),
        out_specs=VMEM,
        scratch_shapes=[
            pltpu.VMEM((4 * rows_down, TB, width), BF),
            pltpu.VMEM((4 * rows_down, TB, width), BF),
            pltpu.VMEM((rows_down * TB, width), BF),
            pltpu.SemaphoreType.DMA((2 * len(blocks),)),
            pltpu.VMEM((recv.size, ROWS, TB), BF),
            pltpu.SemaphoreType.DMA((len(raws),)),
        ],
        compiler_params=BIG,
        name="cross",
    )(me, recv, places, cls, recoup, down, along, *flat, *raws)


def final_kernel(step_size, send, cls, recoup, base, back, out, total, tiles, sems, out_sems):
    rows_down, across = send.shape
    arrive = pltpu.make_async_copy(back, tiles, sems.at[rows_down])
    arrive.start()
    copies, leaves = [], []
    for i in range(rows_down):
        rows = pl.ds(i * TB, TB)
        copies.append(pltpu.make_async_copy(base.at[rows], total.at[rows], sems.at[i]))
        leaves.append(pltpu.make_async_copy(total.at[rows], out.at[rows], out_sems.at[i]))
    for copy in copies:
        copy.start()
    arrive.wait()
    for i in range(rows_down):
        copies[i].wait()
        rows = slice(i * TB, (i + 1) * TB)
        for j in range(across):
            cols = slice(j * TB, (j + 1) * TB)
            turned = lax.dot_general(
                tiles[send[i, j]], recoup[cls[i, j]], (((1,), (1,)), ((), ())), preferred_element_type=F32
            )
            total[rows, cols] = total[rows, cols] + step_size * turned
        leaves[i].start()
    for leave in leaves:
        leave.wait()


def finish(step_size, send, cls, base, back, recoup):
    rows_down = send.shape[0]
    return pl.pallas_call(
        functools.partial(final_kernel, step_size),
        out_shape=jax.ShapeDtypeStruct(base.shape, F32),
        in_specs=[SMEM, SMEM, VMEM, ANY, ANY],
        out_specs=ANY,
        scratch_shapes=[
            pltpu.VMEM(base.shape, F32),
            pltpu.VMEM(back.shape, BF),
            pltpu.SemaphoreType.DMA((rows_down + 1,)),
            pltpu.SemaphoreType.DMA((rows_down,)),
        ],
        compiler_params=BIG,
        name="finish",
    )(send, cls, recoup, base, back)


RIGHT = [(i, (i + 1) % 4) for i in range(4)]
LEFT = [(i, (i + 3) % 4) for i in range(4)]
ACROSS = [(i, (i + 2) % 4) for i in range(4)]


def on_device(gamma_pair, energies, occupancy, recoup, recoup_class, send_slot, recv_slot):
    gamma = gamma_pair[0]
    width = gamma.shape[1]
    across = width // TB
    step_size = 1.0 / math.sqrt(width)
    me = lax.axis_index("tile").astype(jnp.int32).reshape(1)
    send, recv, cls = send_slot[0], recv_slot[0], recoup_class[0]

    arrived = []
    for h in range(CHUNKS):
        buf = pack(h, me, send, cls, gamma, energies, occupancy)
        arrived.append(lax.all_to_all(buf, "chan", split_axis=0, concat_axis=0, tiled=True))
    to_right, to_left = share(me, gamma)
    half = gamma.shape[0] // 2
    from_left = lax.ppermute(to_right, "tile", RIGHT)
    from_right = lax.ppermute(to_left, "tile", LEFT)
    far_a = lax.ppermute(from_left[0:half], "tile", RIGHT)
    far_b = lax.ppermute(from_right[half : 2 * half], "tile", LEFT)
    places = place_tables(
        recv,
        lax.ppermute(recv, "tile", LEFT),
        lax.ppermute(recv, "tile", ACROSS),
        lax.ppermute(recv, "tile", RIGHT),
    )
    base = ladder_base(step_size, me, gamma, from_left, from_right, far_a, far_b, energies, occupancy)

    pieces, codes = [], {}

    def form(kind, chunk, members, raws):
        pair, code = recouple(chunk, across, members, places, recoup, raws, codes.get(kind, ()))
        pieces.append((chunk, members, pair))
        codes.setdefault(kind, code)

    for h in range(CHUNKS):
        own = arrived[h]
        mid = own.shape[0] // 2
        left = lax.ppermute(own, "tile", RIGHT)
        right = lax.ppermute(own, "tile", LEFT)
        opposite = [lax.ppermute(left[0:mid], "tile", RIGHT), lax.ppermute(right[mid:], "tile", LEFT)]
        form("own", h, (0,), ([own],))
        form("side", h, (1, 3), ([right], [left]))
        if h + 1 < CHUNKS:
            form("far", h, (2,), (opposite,))
    crossed = cross(CHUNKS - 1, me, recv, places, recoup, pieces, opposite, codes["far"])
    back = lax.all_to_all(crossed, "chan", split_axis=0, concat_axis=0, tiled=True)
    return finish(step_size, send, cls, base, back, recoup)[None]


def solution(mesh):
    placed = (
        P("chan", "tile", None),
        P("chan", None),
        P("chan", None),
        P(),
        P("chan", "tile", None),
        P("chan", "tile", None),
        P("chan", "tile", None),
    )
    return jax.shard_map(
        on_device, mesh=mesh, in_specs=placed, out_specs=P("chan", "tile", None), check_vma=False
    )
```

```python
import functools
import math

import jax
import jax.numpy as jnp
from jax import lax
from jax.experimental import pallas as pl
from jax.experimental.pallas import tpu as pltpu
from jax.sharding import PartitionSpec as P


BF = jnp.bfloat16
F32 = jnp.float32
TB = 128
META = 8
CHUNKS = 2
ROWS = TB // CHUNKS
SMEM = pl.BlockSpec(memory_space=pltpu.SMEM)
VMEM = pl.BlockSpec(memory_space=pltpu.VMEM)
ANY = pl.BlockSpec(memory_space=pltpu.HBM)
BIG = pltpu.CompilerParams(vmem_limit_bytes=60 << 20)


def coded(energy, occ):
    return jnp.where(occ == 0, energy, jnp.where(occ == 2, -energy, 0.0))


def pack_kernel(chunk, tiles_across, me, send, cls, gamma, energy, occ, buf, row_pieces, col_pieces):
    if chunk == 0:
        value = coded(energy[...], occ[...])
        first = value.astype(BF).astype(F32)
        rest = value - first
        second = rest.astype(BF).astype(F32)
        third = rest - second
        row_pieces[...] = jnp.zeros_like(row_pieces)
        col_pieces[...] = jnp.zeros_like(col_pieces)
        for n, piece in enumerate((first, second, third)):
            row_pieces[n : n + 1, :] = piece
            col_pieces[n + 3 : n + 4, :] = piece
    rows_down = gamma.shape[0] // TB

    def body(k, carry):
        i, j = k // tiles_across, k % tiles_across
        across = pl.ds(pl.multiple_of(j * TB, TB), TB)
        slot = send[i, j]
        buf[slot, 0:ROWS, :] = gamma[pl.ds(pl.multiple_of(i * TB + chunk * ROWS, ROWS), ROWS), across]
        if chunk == 0:
            down = pl.ds(pl.multiple_of((me[0] * rows_down + i) * TB, TB), TB)
            line = lax.broadcasted_iota(jnp.int32, (META, TB), 0)
            head = row_pieces[:, down] + col_pieces[:, across]
            head = head + jnp.where(line == 6, cls[i, j].astype(F32), 0.0)
            buf[slot, ROWS : ROWS + META, :] = head.astype(BF)
        return carry

    lax.fori_loop(0, rows_down * tiles_across, body, 0, unroll=8)


def pack(chunk, me, send, cls, gamma, energy, occ):
    rows = ROWS + (META if chunk == 0 else 0)
    return pl.pallas_call(
        functools.partial(pack_kernel, chunk, gamma.shape[1] // TB),
        out_shape=jax.ShapeDtypeStruct((send.size, rows, TB), BF),
        in_specs=[SMEM] * 3 + [VMEM] * 3,
        out_specs=VMEM,
        scratch_shapes=[pltpu.VMEM((META, gamma.shape[1]), F32)] * 2,
    )(me, send, cls, gamma, energy, occ)


def tables_kernel(own, right, far, left, out):
    across = own.shape[1]
    for n, table in enumerate((own, right, far, left)):

        def body(p, carry, n=n, table=table):
            out[n, table[p // across, p % across]] = p
            return carry

        lax.fori_loop(0, own.shape[0] * across, body, 0, unroll=8)


def place_tables(*tables):
    return pl.pallas_call(
        tables_kernel,
        out_shape=jax.ShapeDtypeStruct((4, tables[0].size), jnp.int32),
        in_specs=[SMEM] * 4,
        out_specs=SMEM,
        name="place_tables",
    )(*tables)


def share_kernel(me, gamma, right, left):
    side = gamma.shape[0]
    half = side // 2

    def block(offset):
        return pl.ds(pl.multiple_of(((me[0] + offset) % 4) * side, side), side)

    own = gamma[:, block(0)]
    right[0:side, :] = own
    left[0:side, :] = own
    right[side : 2 * side, :] = gamma[:, block(3)]
    left[side : 2 * side, :] = gamma[:, block(1)]
    far = gamma[:, block(2)]
    right[2 * side :, :] = far[0:half]
    left[2 * side :, 0:half] = far[0:half, half:]
    left[2 * side :, half:] = far[half:, half:]


def share(me, gamma):
    side = gamma.shape[0]
    shape = jax.ShapeDtypeStruct((2 * side + side // 2, side), BF)
    return pl.pallas_call(
        share_kernel,
        out_shape=[shape, shape],
        in_specs=[SMEM, VMEM],
        out_specs=[VMEM, VMEM],
        name="share_blocks",
    )(me, gamma)


def ladder_kernel(step_size, me, gamma, from_left, from_right, far_a, far_b, energy, occ, base, full, scaled, column):
    side = gamma.shape[0]
    half = side // 2
    width = gamma.shape[1]

    def put(a, b, value, row=0, col=0):
        rows = pl.ds(pl.multiple_of(((me[0] + a) % 4) * side + row, half), value.shape[0])
        cols = pl.ds(pl.multiple_of(((me[0] + b) % 4) * side + col, half), value.shape[1])
        full[rows, cols] = value

    def turn(value):
        return jnp.transpose(value.astype(F32)).astype(BF)

    mine = pl.ds(pl.multiple_of(me[0] * side, side), side)
    full[mine, :] = gamma[...]
    for b in range(1, 4):
        cols = pl.ds(pl.multiple_of(((me[0] + b) % 4) * side, side), side)
        put(b, 0, turn(gamma[:, cols]))
    put(3, 3, from_left[0:side, :])
    put(3, 2, from_left[side : 2 * side, :])
    put(2, 3, turn(from_left[side : 2 * side, :]))
    put(3, 1, from_left[2 * side :, :])
    put(1, 3, turn(from_left[2 * side :, :]))
    put(1, 1, from_right[0:side, :])
    put(1, 2, from_right[side : 2 * side, :])
    put(2, 1, turn(from_right[side : 2 * side, :]))
    for n in range(2):
        piece = from_right[2 * side :, n * half : (n + 1) * half]
        put(1, 3, piece, row=n * half, col=half)
        put(3, 1, turn(piece), row=half, col=n * half)
    put(2, 2, far_a[...])
    put(2, 2, far_b[...], row=half)

    value = coded(energy[...], occ[...])
    column[...] = jnp.transpose(jnp.broadcast_to(value, (8, width)))

    def scale(n, carry):
        rows = pl.ds(pl.multiple_of(n * 64, 64), 64)
        down = column[rows, 0:1]
        ratio = -full[rows, :].astype(F32) / jnp.abs(down - value)
        scaled[rows, :] = jnp.where(down * value < 0.0, ratio, 0.0).astype(BF)
        return carry

    lax.fori_loop(0, width // 64, scale, 0)

    def product(n, carry):
        cols = pl.ds(pl.multiple_of(n * 256, 256), 256)
        total = jnp.dot(scaled[mine, :], full[:, cols], preferred_element_type=F32)
        total = total + jnp.dot(full[mine, :], scaled[:, cols], preferred_element_type=F32)
        base[:, cols] = gamma[:, cols].astype(F32) + step_size * total
        return carry

    lax.fori_loop(0, width // 256, product, 0)


def ladder_base(step_size, me, gamma, from_left, from_right, far_a, far_b, energy, occ):
    width = gamma.shape[1]
    return pl.pallas_call(
        functools.partial(ladder_kernel, step_size),
        out_shape=jax.ShapeDtypeStruct(gamma.shape, F32),
        in_specs=[SMEM] + [VMEM] * 7,
        out_specs=VMEM,
        scratch_shapes=[
            pltpu.VMEM((width, width), BF),
            pltpu.VMEM((width, width), BF),
            pltpu.VMEM((width, 8), F32),
        ],
        compiler_params=BIG,
        name="ladder",
    )(me, gamma, from_left, from_right, far_a, far_b, energy, occ)


def fill_picks(picks, count):
    row = lax.broadcasted_iota(jnp.int32, picks.shape, 0)
    col = lax.broadcasted_iota(jnp.int32, picks.shape, 1)
    kind, line = row // count, col % META
    hit = ((kind == 2) & (line == 6)) | ((kind < 2) & (line >= 3 * kind) & (line < 3 * kind + 3))
    picks[...] = jnp.where((col // META == row % count) & hit, 1.0, 0.0).astype(BF)


def decode(head, picks, down, along, cls):
    count = along.shape[0]
    lines = jnp.dot(picks[...], head, preferred_element_type=F32)
    turned = jnp.transpose(jnp.concatenate([lines[0:count], lines[2 * count :]], axis=0))
    down[...] = turned
    along[...] = lines[count : 2 * count]
    cls[...] = turned[0:META].astype(jnp.int32)


def recouple_block(chunk, across, raw, down, along, cls, places, block, recoup, put):
    count = raw.shape[0]
    for q in range(count):
        column = down[chunk * ROWS : (chunk + 1) * ROWS, q : q + 1]
        line = along[q : q + 1, :]
        tile = raw[q]
        ratio = tile.astype(F32) / (column - line)
        eta = jnp.where(column * line < 0.0, ratio, 0.0).astype(BF)
        both = jnp.concatenate([eta, tile], axis=0)
        done = jnp.dot(both, recoup[cls(q)], preferred_element_type=F32).astype(BF)
        p = places[block, q]
        put(p // across, pl.ds(pl.multiple_of((p % across) * TB, TB), TB), done[0:ROWS], done[ROWS:])


def body_copies(raws, raw, sems):
    copies, start = [], 0
    for n, source in enumerate(raws):
        where = pl.ds(start, source.shape[0])
        start += source.shape[0]
        copies.append(pltpu.make_async_copy(source.at[:, 0:ROWS, :], raw.at[where], sems.at[n]))
    return copies


def head_copies(raws, head, sems):
    copies, start = [], 0
    for n, source in enumerate(raws):
        where = pl.ds(start, source.shape[0])
        start += source.shape[0]
        copies.append(pltpu.make_async_copy(source.at[:, ROWS : ROWS + META, :], head.at[where], sems.at[n]))
    return copies


def recouple_kernel(chunk, across, parts, blocks, places, recoup, *refs):
    groups = len(blocks)
    total = parts * groups
    raws, refs = refs[:total], refs[total:]
    if chunk == 0:
        eta_out, gamma_out, down, along, cls_int, raw, sems, head, picks, cls, head_sems = refs
    else:
        down, along, cls, eta_out, gamma_out, raw, sems = refs
    for n in range(groups):
        mine = raws[n * parts : (n + 1) * parts]
        if chunk == 0:
            for copy in head_copies(mine, head.at[n], head_sems.at[n]):
                copy.start()
        for copy in body_copies(mine, raw.at[n], sems.at[n]):
            copy.start()
    count = raw.shape[1]
    high = eta_out.shape[0] // groups
    if chunk == 0:
        fill_picks(picks, count)
        for n in range(groups):
            for copy in head_copies(raws[n * parts : (n + 1) * parts], head.at[n], head_sems.at[n]):
                copy.wait()
            decode(head[n].reshape(count * META, TB), picks, down.at[n], along.at[n], cls_int.at[n])
        copy = pltpu.make_async_copy(cls_int, cls, head_sems.at[0, 0])
        copy.start()
        copy.wait()

    def group(n, carry):
        block = sum(jnp.where(n == k, b, 0) for k, b in enumerate(blocks))
        for copy in body_copies(raws[:parts], raw.at[n], sems.at[n]):
            copy.wait()

        def put(i, cols, eta_tile, gamma_tile):
            eta_out[n * high + i, :, cols] = eta_tile
            gamma_out[n * high + i, :, cols] = gamma_tile

        recouple_block(
            chunk, across, raw.at[n], down.at[n], along.at[n], lambda q: cls[n, 0, count + q], places, block, recoup, put
        )
        return carry

    lax.fori_loop(0, groups, group, 0)


def recouple(chunk, across, blocks, places, recoup, raws, codes):
    groups, parts = len(blocks), len(raws[0])
    count = sum(raw.shape[0] for raw in raws[0])
    shapes = [jax.ShapeDtypeStruct((groups * count // across, ROWS, across * TB), BF)] * 2
    in_specs = [SMEM, VMEM] + [ANY] * (parts * groups)
    scratch = [pltpu.VMEM((groups, count, ROWS, TB), BF), pltpu.SemaphoreType.DMA((groups, parts))]
    if chunk == 0:
        shapes += [
            jax.ShapeDtypeStruct((groups, TB, 2 * count), F32),
            jax.ShapeDtypeStruct((groups, count, TB), F32),
            jax.ShapeDtypeStruct((groups, META, 2 * count), jnp.int32),
        ]
        scratch += [
            pltpu.VMEM((groups, count, META, TB), BF),
            pltpu.VMEM((3 * count, count * META), BF),
            pltpu.SMEM((groups, META, 2 * count), jnp.int32),
            pltpu.SemaphoreType.DMA((groups, parts)),
        ]
    else:
        in_specs += [VMEM, VMEM, SMEM]
    outs = pl.pallas_call(
        functools.partial(recouple_kernel, chunk, across, parts, blocks),
        out_shape=shapes,
        in_specs=in_specs,
        out_specs=[VMEM] * len(shapes),
        scratch_shapes=scratch,
        compiler_params=BIG,
    )(places, recoup, *[r for group in raws for r in group], *codes)
    return outs[0:2], outs[2:]


def cross_kernel(chunk, blocks, parts, me, recv, places, cls, recoup, down, along, *refs):
    groups = len(set(key for _, _, key, _ in blocks))
    pieces, refs = refs[: 2 * groups], refs[2 * groups :]
    raws, refs = refs[:parts], refs[parts:]
    out, eta, gamma, turned, piece_sems, raw, sems = refs
    rows_down = recv.shape[0]
    width = pieces[0].shape[2]
    late = body_copies(raws, raw, sems)
    eta_copies, gamma_copies = [[] for _ in range(4)], []
    for n, (part, block, key, place) in enumerate(blocks):
        where = pl.ds(((me[0] + block) % 4) * rows_down, rows_down)
        for which, (target, group) in enumerate(((eta, eta_copies[block]), (gamma, gamma_copies))):
            source = pieces[2 * key + which].at[pl.ds(place * rows_down, rows_down)]
            into = target.at[where, pl.ds(part * ROWS, ROWS), :]
            group.append(pltpu.make_async_copy(source, into, piece_sems.at[2 * n + which]))
    for copy in late + gamma_copies + [copy for group in eta_copies for copy in group]:
        copy.start()
    for copy in late:
        copy.wait()
    count = raw.shape[0]
    far = ((me[0] + 2) % 4) * rows_down

    def put(i, cols, eta_tile, gamma_tile):
        eta[far + i, chunk * ROWS : (chunk + 1) * ROWS, cols] = eta_tile
        gamma[far + i, chunk * ROWS : (chunk + 1) * ROWS, cols] = gamma_tile

    recouple_block(
        chunk, width // TB, raw, down.at[0], along.at[0], lambda q: cls[0, 0, count + q], places, 2, recoup, put
    )
    for copy in gamma_copies + eta_copies[0]:
        copy.wait()
    side = rows_down * TB
    mine = pl.ds(me[0] * rows_down, rows_down)
    for i in range(rows_down):
        cols = pl.ds(pl.multiple_of((me[0] * rows_down + i) * TB, TB), TB)
        for k in range(4 * rows_down):
            turned[i * TB : (i + 1) * TB, k * TB : (k + 1) * TB] = jnp.transpose(gamma[k, :, cols])
    step = 2
    turns = rows_down // step

    def body(t, carry):
        for block in range(1, 4):

            @pl.when(t == block * turns)
            def _(block=block):
                for copy in eta_copies[block]:
                    copy.wait()

        n = ((me[0] + t // turns) % 4) * turns + t % turns
        cols = pl.ds(pl.multiple_of(n * step * TB, step * TB), step * TB)
        half = jnp.dot(
            eta[mine].reshape(side, width),
            gamma[:, :, cols].reshape(width, step * TB),
            preferred_element_type=F32,
        )
        other = lax.dot_general(
            turned[...],
            eta[pl.ds(n * step, step)].reshape(step * TB, width),
            (((1,), (1,)), ((), ())),
            preferred_element_type=F32,
        )
        result = (half - other).astype(BF)
        for i in range(rows_down):
            for j in range(step):
                out[recv[i, n * step + j]] = result[i * TB : (i + 1) * TB, j * TB : (j + 1) * TB]
        return carry

    lax.fori_loop(0, 4 * turns, body, 0)


def cross(chunk, me, recv, places, recoup, pieces, raws, codes):
    flat = [array for _, _, pair in pieces for array in pair]
    blocks = tuple(
        (part, block, key, place)
        for key, (part, members, _) in enumerate(pieces)
        for place, block in enumerate(members)
    )
    rows_down, width = recv.shape[0], flat[0].shape[2]
    down, along, cls = codes
    return pl.pallas_call(
        functools.partial(cross_kernel, chunk, blocks, len(raws)),
        out_shape=jax.ShapeDtypeStruct((recv.size, TB, TB), BF),
        in_specs=[SMEM] * 4 + [VMEM] * 3 + [ANY] * (len(flat) + len(raws)),
        out_specs=VMEM,
        scratch_shapes=[
            pltpu.VMEM((4 * rows_down, TB, width), BF),
            pltpu.VMEM((4 * rows_down, TB, width), BF),
            pltpu.VMEM((rows_down * TB, width), BF),
            pltpu.SemaphoreType.DMA((2 * len(blocks),)),
            pltpu.VMEM((recv.size, ROWS, TB), BF),
            pltpu.SemaphoreType.DMA((len(raws),)),
        ],
        compiler_params=BIG,
        name="cross",
    )(me, recv, places, cls, recoup, down, along, *flat, *raws)


def final_kernel(step_size, send, cls, recoup, tiles, base, out, total, sems, out_sems):
    rows_down, across = send.shape
    copies, leaves = [], []
    for i in range(rows_down):
        rows = pl.ds(i * TB, TB)
        copies.append(pltpu.make_async_copy(base.at[rows], total.at[rows], sems.at[i]))
        leaves.append(pltpu.make_async_copy(total.at[rows], out.at[rows], out_sems.at[i]))
    for copy in copies:
        copy.start()
    for i in range(rows_down):
        copies[i].wait()
        rows = slice(i * TB, (i + 1) * TB)
        for j in range(across):
            cols = slice(j * TB, (j + 1) * TB)
            turned = lax.dot_general(
                tiles[send[i, j]], recoup[cls[i, j]], (((1,), (1,)), ((), ())), preferred_element_type=F32
            )
            total[rows, cols] = total[rows, cols] + step_size * turned
        leaves[i].start()
    for leave in leaves:
        leave.wait()


def finish(step_size, send, cls, base, back, recoup):
    rows_down = send.shape[0]
    return pl.pallas_call(
        functools.partial(final_kernel, step_size),
        out_shape=jax.ShapeDtypeStruct(base.shape, F32),
        in_specs=[SMEM, SMEM, VMEM, VMEM, ANY],
        out_specs=ANY,
        scratch_shapes=[
            pltpu.VMEM(base.shape, F32),
            pltpu.SemaphoreType.DMA((rows_down,)),
            pltpu.SemaphoreType.DMA((rows_down,)),
        ],
        compiler_params=BIG,
        name="finish",
    )(send, cls, recoup, pltpu.with_memory_space_constraint(back, pltpu.VMEM), base)


RIGHT = [(i, (i + 1) % 4) for i in range(4)]
LEFT = [(i, (i + 3) % 4) for i in range(4)]
ACROSS = [(i, (i + 2) % 4) for i in range(4)]


def on_device(gamma_pair, energies, occupancy, recoup, recoup_class, send_slot, recv_slot):
    gamma = gamma_pair[0]
    width = gamma.shape[1]
    across = width // TB
    step_size = 1.0 / math.sqrt(width)
    me = lax.axis_index("tile").astype(jnp.int32).reshape(1)
    send, recv, cls = send_slot[0], recv_slot[0], recoup_class[0]

    arrived = []
    for h in range(CHUNKS):
        buf = pack(h, me, send, cls, gamma, energies, occupancy)
        arrived.append(lax.all_to_all(buf, "chan", split_axis=0, concat_axis=0, tiled=True))
    to_right, to_left = share(me, gamma)
    half = gamma.shape[0] // 2
    from_left = lax.ppermute(to_right, "tile", RIGHT)
    from_right = lax.ppermute(to_left, "tile", LEFT)
    far_a = lax.ppermute(from_left[0:half], "tile", RIGHT)
    far_b = lax.ppermute(from_right[half : 2 * half], "tile", LEFT)
    places = place_tables(
        recv,
        lax.ppermute(recv, "tile", LEFT),
        lax.ppermute(recv, "tile", ACROSS),
        lax.ppermute(recv, "tile", RIGHT),
    )
    base = ladder_base(step_size, me, gamma, from_left, from_right, far_a, far_b, energies, occupancy)

    pieces, codes = [], {}

    def form(kind, chunk, members, raws):
        pair, code = recouple(chunk, across, members, places, recoup, raws, codes.get(kind, ()))
        pieces.append((chunk, members, pair))
        codes.setdefault(kind, code)

    for h in range(CHUNKS):
        own = arrived[h]
        mid = own.shape[0] // 2
        left = lax.ppermute(own, "tile", RIGHT)
        right = lax.ppermute(own, "tile", LEFT)
        opposite = [lax.ppermute(left[0:mid], "tile", RIGHT), lax.ppermute(right[mid:], "tile", LEFT)]
        form("own", h, (0,), ([own],))
        form("side", h, (1, 3), ([right], [left]))
        if h + 1 < CHUNKS:
            form("far", h, (2,), (opposite,))
    crossed = cross(CHUNKS - 1, me, recv, places, recoup, pieces, opposite, codes["far"])
    back = lax.all_to_all(crossed, "chan", split_axis=0, concat_axis=0, tiled=True)
    return finish(step_size, send, cls, base, back, recoup)[None]


def solution(mesh):
    placed = (
        P("chan", "tile", None),
        P("chan", None),
        P("chan", None),
        P(),
        P("chan", "tile", None),
        P("chan", "tile", None),
        P("chan", "tile", None),
    )
    return jax.shard_map(
        on_device, mesh=mesh, in_specs=placed, out_specs=P("chan", "tile", None), check_vma=False
    )
```

```python
import functools
import math

import jax
import jax.numpy as jnp
from jax import lax
from jax.experimental import pallas as pl
from jax.experimental.pallas import tpu as pltpu
from jax.sharding import PartitionSpec as P


BF = jnp.bfloat16
F32 = jnp.float32
TB = 128
META = 8
CHUNKS = 2
ROWS = TB // CHUNKS
SMEM = pl.BlockSpec(memory_space=pltpu.SMEM)
VMEM = pl.BlockSpec(memory_space=pltpu.VMEM)
ANY = pl.BlockSpec(memory_space=pltpu.HBM)
BIG = pltpu.CompilerParams(vmem_limit_bytes=60 << 20)


def coded(energy, occ):
    return jnp.where(occ == 0, energy, jnp.where(occ == 2, -energy, 0.0))


def pack_kernel(chunk, tiles_across, me, send, cls, gamma, energy, occ, buf, row_pieces, col_pieces):
    if chunk == 0:
        value = coded(energy[...], occ[...])
        first = value.astype(BF).astype(F32)
        rest = value - first
        second = rest.astype(BF).astype(F32)
        third = rest - second
        row_pieces[...] = jnp.zeros_like(row_pieces)
        col_pieces[...] = jnp.zeros_like(col_pieces)
        for n, piece in enumerate((first, second, third)):
            row_pieces[n : n + 1, :] = piece
            col_pieces[n + 3 : n + 4, :] = piece
    rows_down = gamma.shape[0] // TB

    def body(k, carry):
        i, j = k // tiles_across, k % tiles_across
        across = pl.ds(pl.multiple_of(j * TB, TB), TB)
        slot = send[i, j]
        buf[slot, 0:ROWS, :] = gamma[pl.ds(pl.multiple_of(i * TB + chunk * ROWS, ROWS), ROWS), across]
        if chunk == 0:
            down = pl.ds(pl.multiple_of((me[0] * rows_down + i) * TB, TB), TB)
            line = lax.broadcasted_iota(jnp.int32, (META, TB), 0)
            head = row_pieces[:, down] + col_pieces[:, across]
            head = head + jnp.where(line == 6, cls[i, j].astype(F32), 0.0)
            buf[slot, ROWS : ROWS + META, :] = head.astype(BF)
        return carry

    lax.fori_loop(0, rows_down * tiles_across, body, 0, unroll=8)


def pack(chunk, me, send, cls, gamma, energy, occ):
    rows = ROWS + (META if chunk == 0 else 0)
    return pl.pallas_call(
        functools.partial(pack_kernel, chunk, gamma.shape[1] // TB),
        out_shape=jax.ShapeDtypeStruct((send.size, rows, TB), BF),
        in_specs=[SMEM] * 3 + [VMEM] * 3,
        out_specs=VMEM,
        scratch_shapes=[pltpu.VMEM((META, gamma.shape[1]), F32)] * 2,
    )(me, send, cls, gamma, energy, occ)


def tables_kernel(own, right, far, left, out):
    across = own.shape[1]
    for n, table in enumerate((own, right, far, left)):

        def body(p, carry, n=n, table=table):
            out[n, table[p // across, p % across]] = p
            return carry

        lax.fori_loop(0, own.shape[0] * across, body, 0, unroll=8)


def place_tables(*tables):
    return pl.pallas_call(
        tables_kernel,
        out_shape=jax.ShapeDtypeStruct((4, tables[0].size), jnp.int32),
        in_specs=[SMEM] * 4,
        out_specs=SMEM,
        name="place_tables",
    )(*tables)


def share_kernel(me, gamma, right, left):
    side = gamma.shape[0]
    half = side // 2

    def block(offset):
        return pl.ds(pl.multiple_of(((me[0] + offset) % 4) * side, side), side)

    own = gamma[:, block(0)]
    right[0:side, :] = own
    left[0:side, :] = own
    right[side : 2 * side, :] = gamma[:, block(3)]
    left[side : 2 * side, :] = gamma[:, block(1)]
    far = gamma[:, block(2)]
    right[2 * side :, :] = far[0:half]
    left[2 * side :, 0:half] = far[0:half, half:]
    left[2 * side :, half:] = far[half:, half:]


def share(me, gamma):
    side = gamma.shape[0]
    shape = jax.ShapeDtypeStruct((2 * side + side // 2, side), BF)
    return pl.pallas_call(
        share_kernel,
        out_shape=[shape, shape],
        in_specs=[SMEM, VMEM],
        out_specs=[VMEM, VMEM],
        name="share_blocks",
    )(me, gamma)


def ladder_kernel(step_size, me, gamma, from_left, from_right, far_a, far_b, energy, occ, base, full, scaled, column):
    side = gamma.shape[0]
    half = side // 2
    width = gamma.shape[1]

    def put(a, b, value, row=0, col=0):
        rows = pl.ds(pl.multiple_of(((me[0] + a) % 4) * side + row, half), value.shape[0])
        cols = pl.ds(pl.multiple_of(((me[0] + b) % 4) * side + col, half), value.shape[1])
        full[rows, cols] = value

    def turn(value):
        return jnp.transpose(value.astype(F32)).astype(BF)

    mine = pl.ds(pl.multiple_of(me[0] * side, side), side)
    full[mine, :] = gamma[...]
    for b in range(1, 4):
        cols = pl.ds(pl.multiple_of(((me[0] + b) % 4) * side, side), side)
        put(b, 0, turn(gamma[:, cols]))
    put(3, 3, from_left[0:side, :])
    put(3, 2, from_left[side : 2 * side, :])
    put(2, 3, turn(from_left[side : 2 * side, :]))
    put(3, 1, from_left[2 * side :, :])
    put(1, 3, turn(from_left[2 * side :, :]))
    put(1, 1, from_right[0:side, :])
    put(1, 2, from_right[side : 2 * side, :])
    put(2, 1, turn(from_right[side : 2 * side, :]))
    for n in range(2):
        piece = from_right[2 * side :, n * half : (n + 1) * half]
        put(1, 3, piece, row=n * half, col=half)
        put(3, 1, turn(piece), row=half, col=n * half)
    put(2, 2, far_a[...])
    put(2, 2, far_b[...], row=half)

    value = coded(energy[...], occ[...])
    column[...] = jnp.transpose(jnp.broadcast_to(value, (8, width)))

    def scale(n, carry):
        rows = pl.ds(pl.multiple_of(n * 64, 64), 64)
        down = column[rows, 0:1]
        ratio = -full[rows, :].astype(F32) / jnp.abs(down - value)
        scaled[rows, :] = jnp.where(down * value < 0.0, ratio, 0.0).astype(BF)
        return carry

    lax.fori_loop(0, width // 64, scale, 0)

    def product(n, carry):
        cols = pl.ds(pl.multiple_of(n * 256, 256), 256)
        total = jnp.dot(scaled[mine, :], full[:, cols], preferred_element_type=F32)
        total = total + jnp.dot(full[mine, :], scaled[:, cols], preferred_element_type=F32)
        base[:, cols] = gamma[:, cols].astype(F32) + step_size * total
        return carry

    lax.fori_loop(0, width // 256, product, 0)


def ladder_base(step_size, me, gamma, from_left, from_right, far_a, far_b, energy, occ):
    width = gamma.shape[1]
    return pl.pallas_call(
        functools.partial(ladder_kernel, step_size),
        out_shape=jax.ShapeDtypeStruct(gamma.shape, F32),
        in_specs=[SMEM] + [VMEM] * 7,
        out_specs=VMEM,
        scratch_shapes=[
            pltpu.VMEM((width, width), BF),
            pltpu.VMEM((width, width), BF),
            pltpu.VMEM((width, 8), F32),
        ],
        compiler_params=BIG,
        name="ladder",
    )(me, gamma, from_left, from_right, far_a, far_b, energy, occ)


def fill_picks(picks, count):
    row = lax.broadcasted_iota(jnp.int32, picks.shape, 0)
    col = lax.broadcasted_iota(jnp.int32, picks.shape, 1)
    kind, line = row // count, col % META
    hit = ((kind == 2) & (line == 6)) | ((kind < 2) & (line >= 3 * kind) & (line < 3 * kind + 3))
    picks[...] = jnp.where((col // META == row % count) & hit, 1.0, 0.0).astype(BF)


def decode(head, picks, down, along, cls):
    count = along.shape[0]
    lines = jnp.dot(picks[...], head, preferred_element_type=F32)
    turned = jnp.transpose(jnp.concatenate([lines[0:count], lines[2 * count :]], axis=0))
    down[...] = turned
    along[...] = lines[count : 2 * count]
    cls[...] = turned[0:META].astype(jnp.int32)


def recouple_block(chunk, across, raw, down, along, cls, places, block, recoup, put):
    count = raw.shape[0]
    for q in range(count):
        column = down[chunk * ROWS : (chunk + 1) * ROWS, q : q + 1]
        line = along[q : q + 1, :]
        tile = raw[q]
        ratio = tile.astype(F32) / (column - line)
        eta = jnp.where(column * line < 0.0, ratio, 0.0).astype(BF)
        both = jnp.concatenate([eta, tile], axis=0)
        done = jnp.dot(both, recoup[cls(q)], preferred_element_type=F32).astype(BF)
        p = places[block, q]
        put(p // across, pl.ds(pl.multiple_of((p % across) * TB, TB), TB), done[0:ROWS], done[ROWS:])


def body_copies(raws, raw, sems):
    copies, start = [], 0
    for n, source in enumerate(raws):
        where = pl.ds(start, source.shape[0])
        start += source.shape[0]
        copies.append(pltpu.make_async_copy(source.at[:, 0:ROWS, :], raw.at[where], sems.at[n]))
    return copies


def head_copies(raws, head, sems):
    copies, start = [], 0
    for n, source in enumerate(raws):
        where = pl.ds(start, source.shape[0])
        start += source.shape[0]
        copies.append(pltpu.make_async_copy(source.at[:, ROWS : ROWS + META, :], head.at[where], sems.at[n]))
    return copies


def recouple_kernel(chunk, across, parts, blocks, places, recoup, *refs):
    groups = len(blocks)
    total = parts * groups
    raws, refs = refs[:total], refs[total:]
    if chunk == 0:
        eta_out, gamma_out, down, along, cls_int, raw, sems, head, picks, cls, head_sems = refs
    else:
        down, along, cls, eta_out, gamma_out, raw, sems = refs
    for n in range(groups):
        mine = raws[n * parts : (n + 1) * parts]
        if chunk == 0:
            for copy in head_copies(mine, head.at[n], head_sems.at[n]):
                copy.start()
        for copy in body_copies(mine, raw.at[n], sems.at[n]):
            copy.start()
    count = raw.shape[1]
    high = eta_out.shape[0] // groups
    if chunk == 0:
        fill_picks(picks, count)
        for n in range(groups):
            for copy in head_copies(raws[n * parts : (n + 1) * parts], head.at[n], head_sems.at[n]):
                copy.wait()
            decode(head[n].reshape(count * META, TB), picks, down.at[n], along.at[n], cls_int.at[n])
        copy = pltpu.make_async_copy(cls_int, cls, head_sems.at[0, 0])
        copy.start()
        copy.wait()

    def group(n, carry):
        block = sum(jnp.where(n == k, b, 0) for k, b in enumerate(blocks))
        for copy in body_copies(raws[:parts], raw.at[n], sems.at[n]):
            copy.wait()

        def put(i, cols, eta_tile, gamma_tile):
            eta_out[n * high + i, :, cols] = eta_tile
            gamma_out[n * high + i, :, cols] = gamma_tile

        recouple_block(
            chunk, across, raw.at[n], down.at[n], along.at[n], lambda q: cls[n, 0, count + q], places, block, recoup, put
        )
        return carry

    lax.fori_loop(0, groups, group, 0)


def recouple(chunk, across, blocks, places, recoup, raws, codes):
    groups, parts = len(blocks), len(raws[0])
    count = sum(raw.shape[0] for raw in raws[0])
    shapes = [jax.ShapeDtypeStruct((groups * count // across, ROWS, across * TB), BF)] * 2
    in_specs = [SMEM, VMEM] + [ANY] * (parts * groups)
    scratch = [pltpu.VMEM((groups, count, ROWS, TB), BF), pltpu.SemaphoreType.DMA((groups, parts))]
    if chunk == 0:
        shapes += [
            jax.ShapeDtypeStruct((groups, TB, 2 * count), F32),
            jax.ShapeDtypeStruct((groups, count, TB), F32),
            jax.ShapeDtypeStruct((groups, META, 2 * count), jnp.int32),
        ]
        scratch += [
            pltpu.VMEM((groups, count, META, TB), BF),
            pltpu.VMEM((3 * count, count * META), BF),
            pltpu.SMEM((groups, META, 2 * count), jnp.int32),
            pltpu.SemaphoreType.DMA((groups, parts)),
        ]
    else:
        in_specs += [VMEM, VMEM, SMEM]
    outs = pl.pallas_call(
        functools.partial(recouple_kernel, chunk, across, parts, blocks),
        out_shape=shapes,
        in_specs=in_specs,
        out_specs=[VMEM] * len(shapes),
        scratch_shapes=scratch,
        compiler_params=BIG,
    )(places, recoup, *[r for group in raws for r in group], *codes)
    return outs[0:2], outs[2:]


def cross_kernel(chunk, blocks, parts, me, recv, places, cls, recoup, down, along, *refs):
    groups = len(set(key for _, _, key, _ in blocks))
    pieces, refs = refs[: 2 * groups], refs[2 * groups :]
    raws, refs = refs[:parts], refs[parts:]
    out, eta, gamma, turned, piece_sems, raw, sems = refs
    rows_down = recv.shape[0]
    width = pieces[0].shape[2]
    late = body_copies(raws, raw, sems)
    eta_copies, gamma_copies = [[] for _ in range(4)], []
    for n, (part, block, key, place) in enumerate(blocks):
        where = pl.ds(((me[0] + block) % 4) * rows_down, rows_down)
        for which, (target, group) in enumerate(((eta, eta_copies[block]), (gamma, gamma_copies))):
            source = pieces[2 * key + which].at[pl.ds(place * rows_down, rows_down)]
            into = target.at[where, pl.ds(part * ROWS, ROWS), :]
            group.append(pltpu.make_async_copy(source, into, piece_sems.at[2 * n + which]))
    for copy in late + gamma_copies + [copy for group in eta_copies for copy in group]:
        copy.start()
    for copy in late:
        copy.wait()
    count = raw.shape[0]
    far = ((me[0] + 2) % 4) * rows_down

    def put(i, cols, eta_tile, gamma_tile):
        eta[far + i, chunk * ROWS : (chunk + 1) * ROWS, cols] = eta_tile
        gamma[far + i, chunk * ROWS : (chunk + 1) * ROWS, cols] = gamma_tile

    recouple_block(
        chunk, width // TB, raw, down.at[0], along.at[0], lambda q: cls[0, 0, count + q], places, 2, recoup, put
    )
    for copy in gamma_copies + eta_copies[0]:
        copy.wait()
    side = rows_down * TB
    mine = pl.ds(me[0] * rows_down, rows_down)
    for i in range(rows_down):
        cols = pl.ds(pl.multiple_of((me[0] * rows_down + i) * TB, TB), TB)
        for k in range(4 * rows_down):
            turned[i * TB : (i + 1) * TB, k * TB : (k + 1) * TB] = jnp.transpose(gamma[k, :, cols])
    step = 2
    turns = rows_down // step

    def body(t, carry):
        for block in range(1, 4):

            @pl.when(t == block * turns)
            def _(block=block):
                for copy in eta_copies[block]:
                    copy.wait()

        n = ((me[0] + t // turns) % 4) * turns + t % turns
        cols = pl.ds(pl.multiple_of(n * step * TB, step * TB), step * TB)
        half = jnp.dot(
            eta[mine].reshape(side, width),
            gamma[:, :, cols].reshape(width, step * TB),
            preferred_element_type=F32,
        )
        other = lax.dot_general(
            turned[...],
            eta[pl.ds(n * step, step)].reshape(step * TB, width),
            (((1,), (1,)), ((), ())),
            preferred_element_type=F32,
        )
        result = (half - other).astype(BF)
        for i in range(rows_down):
            for j in range(step):
                out[recv[i, n * step + j]] = result[i * TB : (i + 1) * TB, j * TB : (j + 1) * TB]
        return carry

    lax.fori_loop(0, 4 * turns, body, 0)


def cross(chunk, me, recv, places, recoup, pieces, raws, codes):
    flat = [array for _, _, pair in pieces for array in pair]
    blocks = tuple(
        (part, block, key, place)
        for key, (part, members, _) in enumerate(pieces)
        for place, block in enumerate(members)
    )
    rows_down, width = recv.shape[0], flat[0].shape[2]
    down, along, cls = codes
    return pl.pallas_call(
        functools.partial(cross_kernel, chunk, blocks, len(raws)),
        out_shape=jax.ShapeDtypeStruct((recv.size, TB, TB), BF),
        in_specs=[SMEM] * 4 + [VMEM] * 3 + [ANY] * (len(flat) + len(raws)),
        out_specs=VMEM,
        scratch_shapes=[
            pltpu.VMEM((4 * rows_down, TB, width), BF),
            pltpu.VMEM((4 * rows_down, TB, width), BF),
            pltpu.VMEM((rows_down * TB, width), BF),
            pltpu.SemaphoreType.DMA((2 * len(blocks),)),
            pltpu.VMEM((recv.size, ROWS, TB), BF),
            pltpu.SemaphoreType.DMA((len(raws),)),
        ],
        compiler_params=BIG,
        name="cross",
    )(me, recv, places, cls, recoup, down, along, *flat, *raws)


def final_kernel(step_size, send, cls, recoup, tiles, base, out, total, sems, out_sems):
    rows_down, across = send.shape
    copies, leaves = [], []
    for i in range(rows_down):
        rows = pl.ds(i * TB, TB)
        copies.append(pltpu.make_async_copy(base.at[rows], total.at[rows], sems.at[i]))
        leaves.append(pltpu.make_async_copy(total.at[rows], out.at[rows], out_sems.at[i]))
    for copy in copies:
        copy.start()
    for i in range(rows_down):
        copies[i].wait()
        rows = slice(i * TB, (i + 1) * TB)
        for j in range(across):
            cols = slice(j * TB, (j + 1) * TB)
            turned = lax.dot_general(
                tiles[send[i, j]], recoup[cls[i, j]], (((1,), (1,)), ((), ())), preferred_element_type=F32
            )
            total[rows, cols] = total[rows, cols] + step_size * turned
        leaves[i].start()
    for leave in leaves:
        leave.wait()


def finish(step_size, send, cls, base, back, recoup):
    rows_down = send.shape[0]
    return pl.pallas_call(
        functools.partial(final_kernel, step_size),
        out_shape=jax.ShapeDtypeStruct(base.shape, F32),
        in_specs=[SMEM, SMEM, VMEM, VMEM, ANY],
        out_specs=ANY,
        scratch_shapes=[
            pltpu.VMEM(base.shape, F32),
            pltpu.SemaphoreType.DMA((rows_down,)),
            pltpu.SemaphoreType.DMA((rows_down,)),
        ],
        compiler_params=BIG,
        name="finish",
    )(send, cls, recoup, pltpu.with_memory_space_constraint(back, pltpu.VMEM), base)


RIGHT = [(i, (i + 1) % 4) for i in range(4)]
LEFT = [(i, (i + 3) % 4) for i in range(4)]
ACROSS = [(i, (i + 2) % 4) for i in range(4)]


def on_device(gamma_pair, energies, occupancy, recoup, recoup_class, send_slot, recv_slot):
    gamma = gamma_pair[0]
    width = gamma.shape[1]
    across = width // TB
    step_size = 1.0 / math.sqrt(width)
    me = lax.axis_index("tile").astype(jnp.int32).reshape(1)
    send, recv, cls = send_slot[0], recv_slot[0], recoup_class[0]

    arrived = []
    for h in range(CHUNKS):
        buf = pack(h, me, send, cls, gamma, energies, occupancy)
        arrived.append(lax.all_to_all(buf, "chan", split_axis=0, concat_axis=0, tiled=True))
    to_right, to_left = share(me, gamma)
    half = gamma.shape[0] // 2
    from_left = lax.ppermute(to_right, "tile", RIGHT)
    from_right = lax.ppermute(to_left, "tile", LEFT)
    far_a = lax.ppermute(from_left[0:half], "tile", RIGHT)
    far_b = lax.ppermute(from_right[half : 2 * half], "tile", LEFT)
    places = place_tables(
        recv,
        lax.ppermute(recv, "tile", LEFT),
        lax.ppermute(recv, "tile", ACROSS),
        lax.ppermute(recv, "tile", RIGHT),
    )
    base = ladder_base(step_size, me, gamma, from_left, from_right, far_a, far_b, energies, occupancy)

    pieces, codes = [], {}

    def form(kind, chunk, members, raws):
        pair, code = recouple(chunk, across, members, places, recoup, raws, codes.get(kind, ()))
        pieces.append((chunk, members, pair))
        codes.setdefault(kind, code)

    for h in range(CHUNKS):
        own = arrived[h]
        mid = own.shape[0] // 2
        fore = own[0:mid], own[mid:]
        left_fore = lax.ppermute(fore[0], "tile", RIGHT)
        right_fore = lax.ppermute(fore[1], "tile", LEFT)
        left_aft = lax.ppermute(fore[1], "tile", RIGHT)
        right_aft = lax.ppermute(fore[0], "tile", LEFT)
        opposite = [lax.ppermute(left_fore, "tile", RIGHT), lax.ppermute(right_fore, "tile", LEFT)]
        form("own", h, (0,), ([own],))
        form("side", h, (1, 3), ([right_aft, right_fore], [left_fore, left_aft]))
        if h + 1 < CHUNKS:
            form("far", h, (2,), (opposite,))
    crossed = cross(CHUNKS - 1, me, recv, places, recoup, pieces, opposite, codes["far"])
    back = lax.all_to_all(crossed, "chan", split_axis=0, concat_axis=0, tiled=True)
    return finish(step_size, send, cls, base, back, recoup)[None]


def solution(mesh):
    placed = (
        P("chan", "tile", None),
        P("chan", None),
        P("chan", None),
        P(),
        P("chan", "tile", None),
        P("chan", "tile", None),
        P("chan", "tile", None),
    )
    return jax.shard_map(
        on_device, mesh=mesh, in_specs=placed, out_specs=P("chan", "tile", None), check_vma=False
    )
```
